256 devices in a mesh: img: 32 (over z, y_hi, core), ch: 8 (over x, y_lo).
Axes of the slice: x: 4, y: 4 (y_hi: 2, y_lo: 2; y = y_hi * 2 + y_lo), z: 8, core: 2. Of those that a mesh axis runs over, the one named last changes fastest.
Arguments:
- activations: bfloat16 [384, 56, 2048], P('img', None, 'ch'), may hold values from -6 to 6
- filters: bfloat16 [3, 3, 2048, 4096], P(None, None, 'img', 'ch'), may hold values from -0.046875 to 0.046875
- channel_bias: float32 [4096], P('ch'), may hold values from -3 to 3
Outputs:
- convolved: bfloat16 [384, 56, 4096], P('img', None, 'ch')
The draws below stay inside these ranges and needn't reach their ends.
All inputs are finite; a program needn't handle non-finite values.
Results may differ from the reference program's by a relative error of at most 0.001.
Values may be sent and summed in bfloat16 or wider, within the bound.
A program may use at most 128 MiB of HBM per device.

```python
import jax
import jax.numpy as jnp

CIN = 2048
COUT = 4096
SIDE = 56
ROWS = 384


def block_levels(own_key, shape, cuts, smallest, largest):
    factor_of = 1.0
    for position, blocks in cuts:
        steps = jax.random.uniform(jax.random.fold_in(jax.random.fold_in(own_key, 6), position), (blocks,), jnp.float32, smallest / len(cuts), largest / len(cuts))
        factor_of = factor_of * jnp.repeat(jnp.exp(steps), shape[position] // blocks).reshape((-1,) + (1,) * (len(shape) - 1 - position))
    return factor_of


def normal_values(rng, dims, deviation, reach, pieces=(), kind=jnp.bfloat16):
    result = deviation * jax.random.normal(rng, dims, jnp.float32)
    if pieces:
        result = result * block_levels(rng, dims, pieces, -0.22, 0.18)
    return jnp.clip(result, -reach, reach).astype(kind)


def setup_inputs(seed: int = 0) -> dict:
    splits = jax.random.split(jax.random.key(seed), 4)
    activations = normal_values(splits[0], (ROWS, SIDE, CIN), 1.0, 6.0, ((0, 32), (2, 8)))
    filters = normal_values(splits[1], (3, 3, CIN, COUT), (9 * CIN) ** -0.5, 0.046875, ((2, 32), (3, 8)))
    channel_bias = normal_values(splits[2], (COUT,), 0.5, 3.0, ((0, 8),), jnp.float32)
    return {"activations": activations, "filters": filters, "channel_bias": channel_bias}


def reference(activations, filters, channel_bias):
    row_count = activations.shape[0]
    global_rows = jnp.arange(row_count, dtype=jnp.int32)
    above_mask = (global_rows % SIDE != 0).astype(activations.dtype)
    below_mask = ((global_rows + 1) % SIDE != 0).astype(activations.dtype)
    padded = jnp.pad(activations, ((1, 1), (1, 1), (0, 0)))
    shifted = [padded[:row_count] * above_mask[:, None, None], padded[1:row_count + 1], padded[2:] * below_mask[:, None, None]]
    accumulated = jnp.zeros((row_count * SIDE, filters.shape[3]), jnp.float32)
    for vertical in range(3):
        for horizontal in range(3):
            operand = shifted[vertical][:, horizontal:horizontal + SIDE, :].reshape(row_count * SIDE, -1)
            accumulated = accumulated + jnp.dot(operand, filters[vertical, horizontal], preferred_element_type=jnp.float32)
    output = accumulated + channel_bias[None, :].astype(jnp.float32)
    return output.astype(jnp.bfloat16).reshape(row_count, SIDE, -1)
```

```python
import jax
import jax.numpy as jnp
from jax import lax
from jax.experimental import pallas as pl
from jax.experimental.pallas import tpu as pltpu
from jax.sharding import PartitionSpec as P

MESH = pl.DeviceIdType.MESH
SIDE = 56
ROWS = 384
WIDE = 64
OFFS = (0, -1, 1, 2)

NAMES = ["wx0", "wx1", "hz", "o0", "o1", "a1m", "a1p", "a1hm", "a1hp"]
NAMES += [f"wp{j}q{q}" for j in range(1, 5) for q in range(4)]
NAMES += [f"ws{j}q{q}" for j in range(1, 4) for q in range(4)]
NAMES += [f"wb{t}q{q}" for t in range(8) for q in range(4)]
NAMES += [f"a2{u}{k}" for u in range(4) for k in ("m", "p", "hm", "hp")]
CHUNKS = ("01", "00", "31", "11", "30", "10", "21", "20")
NAMES += [f"{k}{chunk}" for chunk in CHUNKS for k in "ef"]
INDEX = {name: i for i, name in enumerate(NAMES)}

GROUPS = ['halo', 'wx0 wp1q0 ws1q0', 'wp1q2 ws1q2', 'wx1 wp1q1 ws1q1', 'a20m a20p', 'wp2q0 ws2q0 wb0', 'a1m a1p E01', 'wp2q2 ws2q2', 'wp1q3 ws1q3 a20hm a20hp X01', 'a1hp a1hm E00 wb1 wb5', '', 'wp2q1 ws2q1 X00', '', 'a21m a21p', 'wp3q0 ws3q0', 'a22m a22p E31 E11', '', 'wp3q2 ws3q2 X31 X11', '', 'wp2q3 ws2q3 a23m a23p', '', 'wb2 wb6 a21hm a21hp E30', '', 'wp3q1 ws3q1 a22hm a22hp E10 E21 X30', '', 'a23hm a23hp E20 wp4q0 X10 X21', '', 'wp4q2 wp3q3 ws3q3 X20', '', 'wb3 wb7 wp4q1', '']
ORDER = " ".join(GROUPS).split()


def group_of(*names):
    return max(i for i, group in enumerate(GROUPS) for name in group.split() if name in names)


FILTERS_AT = [group_of("wb0"), group_of("wb1", "wb5"), group_of("wb2", "wb6"), group_of("wb3", "wb7"), len(GROUPS)]


def blocks_of(core, dx, dy):
    if core == 0:
        if dx == 0:
            return ["a1m", "a1p"] if dy else ["a1hm", "a1hp"]
        kinds = {3: ("m",), 1: ("p",), 2: ("hm", "hp")}[dx]
        return [f"a2{u}{k}" for u in ((1, 2) if dy else (0, 3)) for k in kinds]
    u = {0: 0, 3: 1, 1: 2, 2: 3}[dx]
    return [f"a2{u}{k}" for k in (("m", "p") if dy else ("hm", "hp"))]


for chunk in CHUNKS:
    need = blocks_of(0, *map(int, chunk)) + blocks_of(1, *map(int, chunk))
    assert all(ORDER.index(name) < ORDER.index("E" + chunk) for name in need)
    assert ORDER.index("E" + chunk) < ORDER.index("X" + chunk)


def kernel(a_ref, w_ref, b_ref, o_ref, abuf, wbuf, acc, ost, send_sem, recv_sem, local_sem):
    img = lax.axis_index("img")
    ch = lax.axis_index("ch")
    z, yh, c = img // 4, (img // 2) % 2, img % 2
    x, y = ch // 2, yh * 2 + ch % 2
    d = 1 - 2 * c

    def dev(px, py, pz, pc):
        px, py, pz = (px + 8) % 4, (py + 8) % 4, (pz + 16) % 8
        return ((pz * 2 + py // 2) * 2 + pc, px * 2 + py % 2)

    sibling = dev(x, y, z, 1 - c)
    partner = dev(x, y + 2, z, c)
    z_next, z_prev = dev(x, y, z + d, c), dev(x, y, z - d, c)

    def first(e):
        return dev(x + c * e, y + (1 - c) * e, z, c)

    def second(e):
        return dev(x + (1 - c) * e, y + c * e, z, c)

    across = dev(x, y, z - d, 1 - c)

    def slot(u, v, lo=1, hi=14):
        px = (x + c * u + (1 - c) * v + 8) % 4
        py = (y + (1 - c) * u + c * v + 8) % 4
        return abuf.at[py // 2, px * 2 + py % 2, pl.ds(lo, hi - lo), pl.ds(0, SIDE)]

    def edge(side, dx, dy, row):
        k = (x + dx) % 4 * 2 + (y + dy) % 2
        return abuf.at[side, k, pl.ds(row, 1), pl.ds(0, SIDE)]

    def piece(dz, q, core):
        at = ((yh if q % 2 == 0 else 1 - yh) * 2 + core) * 64
        return wbuf.at[(z + dz + 16) % 8, q // 2, :, :, pl.ds(pl.multiple_of(at, 64), 64), :]

    def columns(side, n):
        return pl.ds(pl.multiple_of(side * 256 + n * 128, 128), 128)

    def half(side, n):
        return w_ref.at[:, :, :, columns(side, n)]

    def rows_out(side, n):
        return o_ref.at[:, :, columns(side, n)]

    def off(t):
        return -d * t if t <= 4 else d * (t - 4)

    def spec(name):
        if name in ("wx0", "wx1"):
            n = int(name[2])
            return half(1 - yh, n), piece(0, 2 * n, c), partner, piece(0, 2 * n + 1, c)
        if name == "hz":
            return a_ref.at[pl.ds(c * 11, 1)], slot(0, 0, 13, 14), across, slot(0, 0, 13, 14)
        if name[0] in "ef":
            both, dx, dy = slice(None), int(name[1]), int(name[2])
            if name[0] == "e":
                return (edge(both, dx, dy, 12 - 11 * c), edge(both, dx, dy, 14 + c), sibling,
                        edge(both, dx, dy, 15 - c))
            return edge(1 - c, dx, dy, 1 + 11 * c), edge(c, dx, dy, 15 - c), sibling, edge(1 - c, dx, dy, 14 + c)
        if name in ("o0", "o1"):
            n = int(name[1])
            return ost.at[0, n], rows_out(yh, n), partner, rows_out(1 - yh, n)
        if name[0] == "w":
            j, q = int(name[2]), int(name[4])
            if name[1] == "b":
                src, device, mine = piece(off(j), q, c), sibling, piece(-off(j), q, 1 - c)
            else:
                e = -d if name[1] == "p" else d
                src, device, mine = piece(e * (j - 1), q, c), (z_next if name[1] == "p" else z_prev), piece(e * j, q, c)
            own = q % 2 == 0 and j == (0 if name[1] == "b" else 1)
            return half(yh, q // 2) if own else src, src, device, mine
        if name.startswith("a1"):
            k, ring, at = name[2:], first, (lambda e, lo, hi: slot(e, 0, lo, hi))
        else:
            u, k, ring = OFFS[int(name[2])], name[3:], second
            at = lambda e, lo, hi: slot(u, e, lo, hi)
        e, lo, hi, got = {"m": (0, 1, 14, -1), "p": (0, 1, 14, 1), "hm": (-1, 1, 8, 2), "hp": (1, 8, 14, 2)}[k]
        return at(e, lo, hi), at(e, lo, hi), ring(1 if k[-1] == "m" else -1), at(got, lo, hi)

    def copy(name):
        src, dst, device, _ = spec(name)
        i = INDEX[name]
        return pltpu.make_async_remote_copy(
            src_ref=src, dst_ref=dst, send_sem=send_sem.at[i], recv_sem=recv_sem.at[i],
            device_id=device, device_id_type=MESH)

    def start(*names):
        for name in names:
            copy(name).start()

    def arrive(*names):
        for name in names:
            _, _, device, mine = spec(name)
            i = INDEX[name]
            pltpu.make_async_remote_copy(
                src_ref=mine, dst_ref=mine, send_sem=send_sem.at[i], recv_sem=recv_sem.at[i],
                device_id=device, device_id_type=MESH).wait_recv()

    own_a = pltpu.make_async_copy(a_ref, slot(0, 0, 1, 13), local_sem.at[0])
    own_w = [pltpu.make_async_copy(half(yh, n), piece(0, 2 * n, c), local_sem.at[1 + n]) for n in range(2)]

    def event(name):
        if name == "halo":
            own_a.wait()
            arrive("hz")
            start("a1m", "a1p", "a20m", "a20p")
            return
        if name[0] == "E":
            start("e" + name[1:], "f" + name[1:])
            return
        if name[0] == "X":
            arrive("e" + name[1:], "f" + name[1:])
            return
        if name[:2] == "wb":
            if name == "wb0":
                own_w[0].wait()
                own_w[1].wait()
            arrive(*[f"{name}q{q}" for q in range(4)])
            return
        arrive(name)
        if name[:2] == "wx":
            q = int(name[2]) * 2 + 1
            start(f"wp1q{q}", f"ws1q{q}", f"wb0q{q}")
        elif name[0] == "w":
            j, q = int(name[2]), name[4]
            if j < (4 if name[1] == "p" else 3):
                start(f"w{name[1]}{j + 1}q{q}")
            start(f"wb{j if name[1] == 'p' else j + 4}q{q}")
        elif name in ("a1m", "a1p"):
            u = 1 if name == "a1m" else 2
            start(f"a1h{name[2]}", f"a2{u}m", f"a2{u}p")
        elif name == "a1hm":
            start("a23m", "a23p")
        elif name[:2] == "a2" and len(name) == 4:
            start(f"{name[:3]}h{name[3]}")

    barrier = pltpu.get_barrier_semaphore()
    peers = [sibling, partner, z_next, z_prev, first(1), first(-1), second(1), second(-1), across]
    for peer in peers:
        pl.semaphore_signal(barrier, inc=1, device_id=peer, device_id_type=MESH)
    pl.semaphore_wait(barrier, len(peers))

    start("hz", "wx0", "wx1", "wp1q0", "ws1q0", "wp1q2", "ws1q2")
    own_a.start()
    own_w[0].start()
    own_w[1].start()
    start("wb0q0", "wb0q2")

    @pl.loop(0, 24)
    def _(r):
        m = pl.ds(pl.multiple_of(r * WIDE, WIDE), WIDE)
        acc[:, m, :] = jnp.zeros((3, WIDE, 256), jnp.float32)

    @pl.loop(0, 16)
    def _(s):
        abuf[s // 8, s % 8, 0] = jnp.zeros((WIDE, 256), jnp.bfloat16)

    keys = []
    for k in range(8):
        dz, dx, dy = (k - z + 8) % 8, (k // 2 - x + 4) % 4, (k + y) % 2
        far = jnp.where(dz > 4, 8 - dz, dz)
        filters = sum(jnp.where(far == j, FILTERS_AT[j], 0) for j in range(5))
        blocks = sum(
            jnp.where((dx == int(chunk[0])) & (dy == int(chunk[1])), group_of("X" + chunk), 0) for chunk in CHUNKS)
        keys.append(jnp.maximum(filters, blocks) * 8 + k)
    ranks = [sum(jnp.where(other < key, 1, 0) for other in keys) for key in keys]
    ordered = [sum(jnp.where(rank == i, key, 0) for rank, key in zip(ranks, keys)) for i in range(8)]

    def operands_of(k, block):
        def operand(a):
            picked = []
            for r in range(12):
                g = ((z * 2 + block) * 2 + c) * 12 + r
                at, row = block, r + a
                if a == 0:
                    if r == 0:
                        at, row = jnp.where(block == 0, 1 - c, 1), jnp.where(block == 0, 13 + c, 14)
                    row = jnp.where(g % SIDE == 0, 0, row)
                if a == 2:
                    if r == 11:
                        at, row = jnp.where(block == 0, 0, 1 - c), jnp.where(block == 0, 15, 15 - 2 * c)
                    row = jnp.where(((g + 1) % SIDE == 0) | (g + 1 == ROWS), 0, row)
                picked.append(abuf[at, k, row])
            return jnp.concatenate(picked, axis=0)

        return [operand(a) for a in range(3)]

    def rows_of(block):
        return pl.ds(pl.multiple_of(block * 12 * WIDE, WIDE), 12 * WIDE)

    def dots(operands, weights):
        total = jnp.dot(operands[0], weights(0), preferred_element_type=jnp.float32)
        total += jnp.dot(operands[1], weights(1), preferred_element_type=jnp.float32)
        total += jnp.dot(operands[2], weights(2), preferred_element_type=jnp.float32)
        return total

    def compute(k, block):
        operands, m = operands_of(k, block), rows_of(block)
        for b in range(3):
            acc[b, m] += dots(operands, lambda a: jnp.concatenate([wbuf[k, n, a, b] for n in range(2)], axis=1))

    def compute_last(k, block, n):
        operands, m = operands_of(k, block), rows_of(block)
        total = dots(operands, lambda a: jnp.concatenate([wbuf[k, n, a, b] for b in range(3)], axis=1))
        for b in range(3):
            acc[b, m, columns(0, n)] += total[:, b * 128 : b * 128 + 128]

    column = lax.broadcasted_iota(jnp.int32, (WIDE, 128), 0)

    def finish(place, block, n):
        bias = b_ref[:, columns(yh, n)]

        @pl.loop(0, 12)
        def _(r):
            m = pl.ds(pl.multiple_of((block * 12 + r) * WIDE, WIDE), WIDE)
            left = jnp.where(column == 0, 0.0, pltpu.roll(acc[0, m, columns(0, n)], 1, 0))
            right = jnp.where(column == SIDE - 1, 0.0, pltpu.roll(acc[2, m, columns(0, n)], WIDE - 1, 0))
            value = acc[1, m, columns(0, n)] + left + right + bias
            ost[place, n, r] = value[:SIDE].astype(jnp.bfloat16)

    def dispatch(step, lo, hi):
        if hi - lo == 1:
            for name in GROUPS[lo].split():
                event(name)
            return
        mid = (lo + hi) // 2

        @pl.when(step < mid)
        def _():
            dispatch(step, lo, mid)

        @pl.when(step >= mid)
        def _():
            dispatch(step, mid, hi)

    def turn(step, done):
        @pl.when(step < len(GROUPS))
        def _():
            dispatch(step, 0, len(GROUPS))

        key = sum(jnp.where(done // 2 == i, ordered[i], 0) for i in range(8))
        ready = (done < 14) & (key // 8 <= step)

        @pl.when(ready)
        def _():
            compute(key % 8, jnp.where(done % 2 == 0, 1 - yh, yh))

        return done + jnp.where(ready, 1, 0)

    lax.fori_loop(0, len(GROUPS) + 13, turn, 0)

    outs = [pltpu.make_async_copy(ost.at[1, n], rows_out(yh, n), local_sem.at[3 + n]) for n in range(2)]

    @pl.loop(0, 4)
    def _(t):
        n, place = t // 2, t % 2

        @pl.when(t == 0)
        def _():
            arrive("wb4q0", "wb4q1")

        @pl.when(t == 2)
        def _():
            event("wp4q3")
            arrive("wb4q2", "wb4q3")

        block = jnp.where(place == 0, 1 - yh, yh)
        compute_last((z + 4) % 8, block, n)
        finish(place, block, n)
        for i in range(2):

            @pl.when(t == 2 * i)
            def _():
                start(f"o{i}")

            @pl.when(t == 2 * i + 1)
            def _():
                outs[i].start()

    arrive("o0", "o1")
    for name in NAMES:
        copy(name).wait_send()
    outs[0].wait()
    outs[1].wait()


def local(activations, filters, channel_bias):
    out_local = filters.shape[3]
    return pl.pallas_call(
        kernel,
        out_shape=jax.ShapeDtypeStruct((12, SIDE, out_local), jnp.bfloat16),
        in_specs=[
            pl.BlockSpec(memory_space=pl.ANY),
            pl.BlockSpec(memory_space=pl.ANY),
            pl.BlockSpec(memory_space=pltpu.VMEM),
        ],
        out_specs=pl.BlockSpec(memory_space=pl.ANY),
        scratch_shapes=[
            pltpu.VMEM((2, 8, 16, WIDE, 256), jnp.bfloat16),
            pltpu.VMEM((8, 2, 3, 3, 256, 128), jnp.bfloat16),
            pltpu.VMEM((3, 24 * WIDE, 256), jnp.float32),
            pltpu.VMEM((2, 2, 12, SIDE, 128), jnp.bfloat16),
            pltpu.SemaphoreType.DMA((len(NAMES),)),
            pltpu.SemaphoreType.DMA((len(NAMES),)),
            pltpu.SemaphoreType.DMA((5,)),
        ],
        compiler_params=pltpu.CompilerParams(collective_id=0, has_side_effects=True),
    )(activations, filters, channel_bias.reshape(1, out_local))


def solution(mesh):
    placed = (P("img", None, "ch"), P(None, None, "img", "ch"), P("ch"))
    return jax.shard_map(
        local, mesh=mesh, in_specs=placed, out_specs=P("img", None, "ch"), check_vma=False
    )
```

```python
import jax
import jax.numpy as jnp
from jax import lax
from jax.experimental import pallas as pl
from jax.experimental.pallas import tpu as pltpu
from jax.sharding import PartitionSpec as P

MESH = pl.DeviceIdType.MESH
SIDE = 56
ROWS = 384
WIDE = 64
OFFS = (0, -1, 1, 2)

NAMES = ["wx0", "wx1", "hz", "o0", "o1", "a1m", "a1p", "a1hm", "a1hp"]
NAMES += [f"wp{j}q{q}" for j in range(1, 5) for q in range(4)]
NAMES += [f"ws{j}q{q}" for j in range(1, 4) for q in range(4)]
NAMES += [f"wb{t}q{q}" for t in range(8) for q in range(4)]
NAMES += [f"a2{u}{k}" for u in range(4) for k in ("m", "p", "hm", "hp")]
CHUNKS = ("01", "00", "31", "11", "30", "10", "21", "20")
NAMES += [f"{k}{chunk}" for chunk in CHUNKS for k in "ef"]
INDEX = {name: i for i, name in enumerate(NAMES)}

GROUPS = ['halo', 'wx0 wp1q0 ws1q0', 'wp1q2 ws1q2', 'wx1 wp1q1 ws1q1', 'a20m a20p', 'wp2q0 ws2q0 wb0', 'a1m a1p E01', 'wp2q2 ws2q2', 'wp1q3 ws1q3 a20hm a20hp X01', 'a1hp a1hm E00 wb1 wb5', '', 'wp2q1 ws2q1 X00', '', 'a21m a21p', 'wp3q0 ws3q0', 'a22m a22p E31 E11', '', 'wp3q2 ws3q2 X31 X11', '', 'wp2q3 ws2q3 a23m a23p', '', 'wb2 wb6 a21hm a21hp E30', '', 'wp3q1 ws3q1 a22hm a22hp E10 E21 X30', '', 'a23hm a23hp E20 wp4q0 X10 X21', '', 'X20', 'wp4q2 wp3q3 ws3q3', '', 'wb3 wb7 wp4q1', '']
ORDER = " ".join(GROUPS).split()


def group_of(*names):
    return max(i for i, group in enumerate(GROUPS) for name in group.split() if name in names)


FILTERS_AT = [group_of("wb0"), group_of("wb1", "wb5"), group_of("wb2", "wb6"), group_of("wb3", "wb7"), len(GROUPS)]


def blocks_of(core, dx, dy):
    if core == 0:
        if dx == 0:
            return ["a1m", "a1p"] if dy else ["a1hm", "a1hp"]
        kinds = {3: ("m",), 1: ("p",), 2: ("hm", "hp")}[dx]
        return [f"a2{u}{k}" for u in ((1, 2) if dy else (0, 3)) for k in kinds]
    u = {0: 0, 3: 1, 1: 2, 2: 3}[dx]
    return [f"a2{u}{k}" for k in (("m", "p") if dy else ("hm", "hp"))]


for chunk in CHUNKS:
    need = blocks_of(0, *map(int, chunk)) + blocks_of(1, *map(int, chunk))
    assert all(ORDER.index(name) < ORDER.index("E" + chunk) for name in need)
    assert ORDER.index("E" + chunk) < ORDER.index("X" + chunk)


def kernel(a_ref, w_ref, b_ref, o_ref, abuf, wbuf, acc, ost, send_sem, recv_sem, local_sem):
    img = lax.axis_index("img")
    ch = lax.axis_index("ch")
    z, yh, c = img // 4, (img // 2) % 2, img % 2
    x, y = ch // 2, yh * 2 + ch % 2
    d = 1 - 2 * c

    def dev(px, py, pz, pc):
        px, py, pz = (px + 8) % 4, (py + 8) % 4, (pz + 16) % 8
        return ((pz * 2 + py // 2) * 2 + pc, px * 2 + py % 2)

    sibling = dev(x, y, z, 1 - c)
    partner = dev(x, y + 2, z, c)
    z_next, z_prev = dev(x, y, z + d, c), dev(x, y, z - d, c)

    def first(e):
        return dev(x + c * e, y + (1 - c) * e, z, c)

    def second(e):
        return dev(x + (1 - c) * e, y + c * e, z, c)

    across = dev(x, y, z - d, 1 - c)

    def slot(u, v, lo=1, hi=14):
        px = (x + c * u + (1 - c) * v + 8) % 4
        py = (y + (1 - c) * u + c * v + 8) % 4
        return abuf.at[py // 2, px * 2 + py % 2, pl.ds(lo, hi - lo), pl.ds(0, SIDE)]

    def edge(side, dx, dy, row):
        k = (x + dx) % 4 * 2 + (y + dy) % 2
        return abuf.at[side, k, pl.ds(row, 1), pl.ds(0, SIDE)]

    def piece(dz, q, core):
        at = ((yh if q % 2 == 0 else 1 - yh) * 2 + core) * 64
        return wbuf.at[(z + dz + 16) % 8, q // 2, :, :, pl.ds(pl.multiple_of(at, 64), 64), :]

    def columns(side, n):
        return pl.ds(pl.multiple_of(side * 256 + n * 128, 128), 128)

    def half(side, n):
        return w_ref.at[:, :, :, columns(side, n)]

    def rows_out(side, n):
        return o_ref.at[:, :, columns(side, n)]

    def off(t):
        return -d * t if t <= 4 else d * (t - 4)

    def spec(name):
        if name in ("wx0", "wx1"):
            n = int(name[2])
            return half(1 - yh, n), piece(0, 2 * n, c), partner, piece(0, 2 * n + 1, c)
        if name == "hz":
            return a_ref.at[pl.ds(c * 11, 1)], slot(0, 0, 13, 14), across, slot(0, 0, 13, 14)
        if name[0] in "ef":
            both, dx, dy = slice(None), int(name[1]), int(name[2])
            if name[0] == "e":
                return (edge(both, dx, dy, 12 - 11 * c), edge(both, dx, dy, 14 + c), sibling,
                        edge(both, dx, dy, 15 - c))
            return edge(1 - c, dx, dy, 1 + 11 * c), edge(c, dx, dy, 15 - c), sibling, edge(1 - c, dx, dy, 14 + c)
        if name in ("o0", "o1"):
            n = int(name[1])
            return ost.at[0, n], rows_out(yh, n), partner, rows_out(1 - yh, n)
        if name[0] == "w":
            j, q = int(name[2]), int(name[4])
            if name[1] == "b":
                src, device, mine = piece(off(j), q, c), sibling, piece(-off(j), q, 1 - c)
            else:
                e = -d if name[1] == "p" else d
                src, device, mine = piece(e * (j - 1), q, c), (z_next if name[1] == "p" else z_prev), piece(e * j, q, c)
            own = q % 2 == 0 and j == (0 if name[1] == "b" else 1)
            return half(yh, q // 2) if own else src, src, device, mine
        if name.startswith("a1"):
            k, ring, at = name[2:], first, (lambda e, lo, hi: slot(e, 0, lo, hi))
        else:
            u, k, ring = OFFS[int(name[2])], name[3:], second
            at = lambda e, lo, hi: slot(u, e, lo, hi)
        e, lo, hi, got = {"m": (0, 1, 14, -1), "p": (0, 1, 14, 1), "hm": (-1, 1, 8, 2), "hp": (1, 8, 14, 2)}[k]
        return at(e, lo, hi), at(e, lo, hi), ring(1 if k[-1] == "m" else -1), at(got, lo, hi)

    def copy(name):
        src, dst, device, _ = spec(name)
        i = INDEX[name]
        return pltpu.make_async_remote_copy(
            src_ref=src, dst_ref=dst, send_sem=send_sem.at[i], recv_sem=recv_sem.at[i],
            device_id=device, device_id_type=MESH)

    def start(*names):
        for name in names:
            copy(name).start()

    def arrive(*names):
        for name in names:
            _, _, device, mine = spec(name)
            i = INDEX[name]
            pltpu.make_async_remote_copy(
                src_ref=mine, dst_ref=mine, send_sem=send_sem.at[i], recv_sem=recv_sem.at[i],
                device_id=device, device_id_type=MESH).wait_recv()

    own_a = pltpu.make_async_copy(a_ref, slot(0, 0, 1, 13), local_sem.at[0])
    own_w = [pltpu.make_async_copy(half(yh, n), piece(0, 2 * n, c), local_sem.at[1 + n]) for n in range(2)]

    def event(name):
        if name == "halo":
            own_a.wait()
            arrive("hz")
            start("a1m", "a1p", "a20m", "a20p")
            return
        if name[0] == "E":
            start("e" + name[1:], "f" + name[1:])
            return
        if name[0] == "X":
            arrive("e" + name[1:], "f" + name[1:])
            return
        if name[:2] == "wb":
            if name == "wb0":
                own_w[0].wait()
                own_w[1].wait()
            arrive(*[f"{name}q{q}" for q in range(4)])
            return
        arrive(name)
        if name[:2] == "wx":
            q = int(name[2]) * 2 + 1
            start(f"wp1q{q}", f"ws1q{q}", f"wb0q{q}")
        elif name[0] == "w":
            j, q = int(name[2]), name[4]
            if j < (4 if name[1] == "p" else 3):
                start(f"w{name[1]}{j + 1}q{q}")
            start(f"wb{j if name[1] == 'p' else j + 4}q{q}")
        elif name in ("a1m", "a1p"):
            u = 1 if name == "a1m" else 2
            start(f"a1h{name[2]}", f"a2{u}m", f"a2{u}p")
        elif name == "a1hm":
            start("a23m", "a23p")
        elif name[:2] == "a2" and len(name) == 4:
            start(f"{name[:3]}h{name[3]}")

    barrier = pltpu.get_barrier_semaphore()
    peers = [sibling, partner, z_next, z_prev, first(1), first(-1), second(1), second(-1), across]
    for peer in peers:
        pl.semaphore_signal(barrier, inc=1, device_id=peer, device_id_type=MESH)
    pl.semaphore_wait(barrier, len(peers))

    start("hz", "wx0", "wx1", "wp1q0", "ws1q0", "wp1q2", "ws1q2")
    own_a.start()
    own_w[0].start()
    own_w[1].start()
    start("wb0q0", "wb0q2")

    @pl.loop(0, 24)
    def _(r):
        m = pl.ds(pl.multiple_of(r * WIDE, WIDE), WIDE)
        acc[:, m, :] = jnp.zeros((3, WIDE, 256), jnp.float32)

    @pl.loop(0, 16)
    def _(s):
        abuf[s // 8, s % 8, 0] = jnp.zeros((WIDE, 256), jnp.bfloat16)

    keys = []
    for k in range(8):
        dz, dx, dy = (k - z + 8) % 8, (k // 2 - x + 4) % 4, (k + y) % 2
        far = jnp.where(dz > 4, 8 - dz, dz)
        filters = sum(jnp.where(far == j, FILTERS_AT[j], 0) for j in range(5))
        blocks = sum(
            jnp.where((dx == int(chunk[0])) & (dy == int(chunk[1])), group_of("X" + chunk), 0) for chunk in CHUNKS)
        keys.append(jnp.maximum(filters, blocks) * 8 + k)
    ranks = [sum(jnp.where(other < key, 1, 0) for other in keys) for key in keys]
    ordered = [sum(jnp.where(rank == i, key, 0) for rank, key in zip(ranks, keys)) for i in range(8)]

    def operands_of(k, block):
        def operand(a):
            picked = []
            for r in range(12):
                g = ((z * 2 + block) * 2 + c) * 12 + r
                at, row = block, r + a
                if a == 0:
                    if r == 0:
                        at, row = jnp.where(block == 0, 1 - c, 1), jnp.where(block == 0, 13 + c, 14)
                    row = jnp.where(g % SIDE == 0, 0, row)
                if a == 2:
                    if r == 11:
                        at, row = jnp.where(block == 0, 0, 1 - c), jnp.where(block == 0, 15, 15 - 2 * c)
                    row = jnp.where(((g + 1) % SIDE == 0) | (g + 1 == ROWS), 0, row)
                picked.append(abuf[at, k, row])
            return jnp.concatenate(picked, axis=0)

        return [operand(a) for a in range(3)]

    def rows_of(block):
        return pl.ds(pl.multiple_of(block * 12 * WIDE, WIDE), 12 * WIDE)

    def dots(operands, weights):
        total = jnp.dot(operands[0], weights(0), preferred_element_type=jnp.float32)
        total += jnp.dot(operands[1], weights(1), preferred_element_type=jnp.float32)
        total += jnp.dot(operands[2], weights(2), preferred_element_type=jnp.float32)
        return total

    def compute(k, block):
        operands, m = operands_of(k, block), rows_of(block)
        for b in range(3):
            acc[b, m] += dots(operands, lambda a: jnp.concatenate([wbuf[k, n, a, b] for n in range(2)], axis=1))

    def compute_last(k, block, n):
        operands, m = operands_of(k, block), rows_of(block)
        total = dots(operands, lambda a: jnp.concatenate([wbuf[k, n, a, b] for b in range(3)], axis=1))
        for b in range(3):
            acc[b, m, columns(0, n)] += total[:, b * 128 : b * 128 + 128]

    column = lax.broadcasted_iota(jnp.int32, (WIDE, 128), 0)

    def finish(place, block, n):
        bias = b_ref[:, columns(yh, n)]

        @pl.loop(0, 12, unroll=3)
        def _(r):
            m = pl.ds(pl.multiple_of((block * 12 + r) * WIDE, WIDE), WIDE)
            left = jnp.where(column == 0, 0.0, pltpu.roll(acc[0, m, columns(0, n)], 1, 0))
            right = jnp.where(column == SIDE - 1, 0.0, pltpu.roll(acc[2, m, columns(0, n)], WIDE - 1, 0))
            value = acc[1, m, columns(0, n)] + left + right + bias
            ost[place, n, r] = value[:SIDE].astype(jnp.bfloat16)

    def dispatch(step, lo, hi):
        if hi - lo == 1:
            for name in GROUPS[lo].split():
                event(name)
            return
        mid = (lo + hi) // 2

        @pl.when(step < mid)
        def _():
            dispatch(step, lo, mid)

        @pl.when(step >= mid)
        def _():
            dispatch(step, mid, hi)

    def turn(step, done):
        @pl.when(step < len(GROUPS))
        def _():
            dispatch(step, 0, len(GROUPS))

        key = sum(jnp.where(done // 2 == i, ordered[i], 0) for i in range(8))
        ready = (done < 14) & (key // 8 <= step)

        @pl.when(ready)
        def _():
            compute(key % 8, jnp.where(done % 2 == 0, 1 - yh, yh))

        return done + jnp.where(ready, 1, 0)

    lax.fori_loop(0, len(GROUPS) + 13, turn, 0)

    outs = [pltpu.make_async_copy(ost.at[1, n], rows_out(yh, n), local_sem.at[3 + n]) for n in range(2)]

    @pl.loop(0, 4)
    def _(t):
        n, place = t // 2, t % 2

        @pl.when(t == 0)
        def _():
            arrive("wb4q0", "wb4q1")

        @pl.when(t == 2)
        def _():
            event("wp4q3")
            arrive("wb4q2", "wb4q3")

        block = jnp.where(place == 0, 1 - yh, yh)
        compute_last((z + 4) % 8, block, n)
        finish(place, block, n)
        for i in range(2):

            @pl.when(t == 2 * i)
            def _():
                start(f"o{i}")

            @pl.when(t == 2 * i + 1)
            def _():
                outs[i].start()

    for name in NAMES:
        if name[0] != "o":
            copy(name).wait_send()
    outs[0].wait()
    outs[1].wait()
    arrive("o0", "o1")
    copy("o0").wait_send()
    copy("o1").wait_send()


def local(activations, filters, channel_bias):
    out_local = filters.shape[3]
    return pl.pallas_call(
        kernel,
        out_shape=jax.ShapeDtypeStruct((12, SIDE, out_local), jnp.bfloat16),
        in_specs=[
            pl.BlockSpec(memory_space=pl.ANY),
            pl.BlockSpec(memory_space=pl.ANY),
            pl.BlockSpec(memory_space=pltpu.VMEM),
        ],
        out_specs=pl.BlockSpec(memory_space=pl.ANY),
        scratch_shapes=[
            pltpu.VMEM((2, 8, 16, WIDE, 256), jnp.bfloat16),
            pltpu.VMEM((8, 2, 3, 3, 256, 128), jnp.bfloat16),
            pltpu.VMEM((3, 24 * WIDE, 256), jnp.float32),
            pltpu.VMEM((2, 2, 12, SIDE, 128), jnp.bfloat16),
            pltpu.SemaphoreType.DMA((len(NAMES),)),
            pltpu.SemaphoreType.DMA((len(NAMES),)),
            pltpu.SemaphoreType.DMA((5,)),
        ],
        compiler_params=pltpu.CompilerParams(collective_id=0, has_side_effects=True),
    )(activations, filters, channel_bias.reshape(1, out_local))


def solution(mesh):
    placed = (P("img", None, "ch"), P(None, None, "img", "ch"), P("ch"))
    return jax.shard_map(
        local, mesh=mesh, in_specs=placed, out_specs=P("img", None, "ch"), check_vma=False
    )
```

```python
import jax
import jax.numpy as jnp
from jax import lax
from jax.experimental import pallas as pl
from jax.experimental.pallas import tpu as pltpu
from jax.sharding import PartitionSpec as P

MESH = pl.DeviceIdType.MESH
SIDE = 56
ROWS = 384
WIDE = 64
OFFS = (0, -1, 1, 2)

NAMES = ["wx0", "wx1", "hz", "o0", "o1", "a1m", "a1p", "a1hm", "a1hp"]
NAMES += [f"wp{j}q{q}" for j in range(1, 5) for q in range(4)]
NAMES += [f"ws{j}q{q}" for j in range(1, 4) for q in range(4)]
NAMES += [f"wb{t}q{q}" for t in range(8) for q in range(4)]
NAMES += [f"a2{u}{k}" for u in range(4) for k in ("m", "p", "hm", "hp")]
CHUNKS = ("01", "00", "31", "11", "30", "10", "21", "20")
NAMES += [f"{k}{chunk}" for chunk in CHUNKS for k in "ef"]
INDEX = {name: i for i, name in enumerate(NAMES)}

GROUPS = ['halo', 'wx0 wp1q0 ws1q0', 'wp1q2 ws1q2', 'wx1 wp1q1 ws1q1', 'a20m a20p', 'wp2q0 ws2q0 wb0', 'a1m a1p E01', 'wp2q2 ws2q2', 'wp1q3 ws1q3 a20hm a20hp X01', 'a1hp a1hm E00 wb1 wb5', '', 'wp2q1 ws2q1 X00', '', 'a21m a21p', 'wp3q0 ws3q0', 'a22m a22p E31 E11', '', 'wp3q2 ws3q2 X31 X11', '', 'wp2q3 ws2q3 a23m a23p', '', 'wb2 wb6 a21hm a21hp E30', '', 'wp3q1 ws3q1 a22hm a22hp E10 E21 X30', '', 'a23hm a23hp E20 wp4q0 X10 X21', '', 'X20', 'wp4q2 wp3q3 ws3q3', '', 'wb3 wb7 wp4q1', '']
ORDER = " ".join(GROUPS).split()


def group_of(*names):
    return max(i for i, group in enumerate(GROUPS) for name in group.split() if name in names)


FILTERS_AT = [group_of("wb0"), group_of("wb1", "wb5"), group_of("wb2", "wb6"), group_of("wb3", "wb7"), len(GROUPS)]


def blocks_of(core, dx, dy):
    if core == 0:
        if dx == 0:
            return ["a1m", "a1p"] if dy else ["a1hm", "a1hp"]
        kinds = {3: ("m",), 1: ("p",), 2: ("hm", "hp")}[dx]
        return [f"a2{u}{k}" for u in ((1, 2) if dy else (0, 3)) for k in kinds]
    u = {0: 0, 3: 1, 1: 2, 2: 3}[dx]
    return [f"a2{u}{k}" for k in (("m", "p") if dy else ("hm", "hp"))]


for chunk in CHUNKS:
    need = blocks_of(0, *map(int, chunk)) + blocks_of(1, *map(int, chunk))
    assert all(ORDER.index(name) < ORDER.index("E" + chunk) for name in need)
    assert ORDER.index("E" + chunk) < ORDER.index("X" + chunk)


def kernel(a_ref, w_ref, b_ref, o_ref, abuf, wbuf, acc, ost, send_sem, recv_sem, local_sem):
    img = lax.axis_index("img")
    ch = lax.axis_index("ch")
    z, yh, c = img // 4, (img // 2) % 2, img % 2
    x, y = ch // 2, yh * 2 + ch % 2
    d = 1 - 2 * c

    def dev(px, py, pz, pc):
        px, py, pz = (px + 8) % 4, (py + 8) % 4, (pz + 16) % 8
        return ((pz * 2 + py // 2) * 2 + pc, px * 2 + py % 2)

    sibling = dev(x, y, z, 1 - c)
    partner = dev(x, y + 2, z, c)
    z_next, z_prev = dev(x, y, z + d, c), dev(x, y, z - d, c)

    def first(e):
        return dev(x + c * e, y + (1 - c) * e, z, c)

    def second(e):
        return dev(x + (1 - c) * e, y + c * e, z, c)

    across = dev(x, y, z - d, 1 - c)

    def slot(u, v, lo=1, hi=14):
        px = (x + c * u + (1 - c) * v + 8) % 4
        py = (y + (1 - c) * u + c * v + 8) % 4
        return abuf.at[py // 2, px * 2 + py % 2, pl.ds(lo, hi - lo), pl.ds(0, SIDE)]

    def edge(side, dx, dy, row):
        k = (x + dx) % 4 * 2 + (y + dy) % 2
        return abuf.at[side, k, pl.ds(row, 1), pl.ds(0, SIDE)]

    def piece(dz, q, core):
        at = ((yh if q % 2 == 0 else 1 - yh) * 2 + core) * 64
        return wbuf.at[(z + dz + 16) % 8, q // 2, :, :, pl.ds(pl.multiple_of(at, 64), 64), :]

    def columns(side, n):
        return pl.ds(pl.multiple_of(side * 256 + n * 128, 128), 128)

    def half(side, n):
        return w_ref.at[:, :, :, columns(side, n)]

    def rows_out(side, n):
        return o_ref.at[:, :, columns(side, n)]

    def off(t):
        return -d * t if t <= 4 else d * (t - 4)

    def spec(name):
        if name in ("wx0", "wx1"):
            n = int(name[2])
            return half(1 - yh, n), piece(0, 2 * n, c), partner, piece(0, 2 * n + 1, c)
        if name == "hz":
            return a_ref.at[pl.ds(c * 11, 1)], slot(0, 0, 13, 14), across, slot(0, 0, 13, 14)
        if name[0] in "ef":
            both, dx, dy = slice(None), int(name[1]), int(name[2])
            if name[0] == "e":
                return (edge(both, dx, dy, 12 - 11 * c), edge(both, dx, dy, 14 + c), sibling,
                        edge(both, dx, dy, 15 - c))
            return edge(1 - c, dx, dy, 1 + 11 * c), edge(c, dx, dy, 15 - c), sibling, edge(1 - c, dx, dy, 14 + c)
        if name in ("o0", "o1"):
            n = int(name[1])
            return ost.at[0, n], rows_out(yh, n), partner, rows_out(1 - yh, n)
        if name[0] == "w":
            j, q = int(name[2]), int(name[4])
            if name[1] == "b":
                src, device, mine = piece(off(j), q, c), sibling, piece(-off(j), q, 1 - c)
            else:
                e = -d if name[1] == "p" else d
                src, device, mine = piece(e * (j - 1), q, c), (z_next if name[1] == "p" else z_prev), piece(e * j, q, c)
            own = q % 2 == 0 and j == (0 if name[1] == "b" else 1)
            return half(yh, q // 2) if own else src, src, device, mine
        if name.startswith("a1"):
            k, ring, at = name[2:], first, (lambda e, lo, hi: slot(e, 0, lo, hi))
        else:
            u, k, ring = OFFS[int(name[2])], name[3:], second
            at = lambda e, lo, hi: slot(u, e, lo, hi)
        e, lo, hi, got = {"m": (0, 1, 14, -1), "p": (0, 1, 14, 1), "hm": (-1, 1, 8, 2), "hp": (1, 8, 14, 2)}[k]
        return at(e, lo, hi), at(e, lo, hi), ring(1 if k[-1] == "m" else -1), at(got, lo, hi)

    def copy(name):
        src, dst, device, _ = spec(name)
        i = INDEX[name]
        return pltpu.make_async_remote_copy(
            src_ref=src, dst_ref=dst, send_sem=send_sem.at[i], recv_sem=recv_sem.at[i],
            device_id=device, device_id_type=MESH)

    def start(*names):
        for name in names:
            copy(name).start()

    def arrive(*names):
        for name in names:
            _, _, device, mine = spec(name)
            i = INDEX[name]
            pltpu.make_async_remote_copy(
                src_ref=mine, dst_ref=mine, send_sem=send_sem.at[i], recv_sem=recv_sem.at[i],
                device_id=device, device_id_type=MESH).wait_recv()

    own_a = pltpu.make_async_copy(a_ref, slot(0, 0, 1, 13), local_sem.at[0])
    own_w = [pltpu.make_async_copy(half(yh, n), piece(0, 2 * n, c), local_sem.at[1 + n]) for n in range(2)]

    def event(name):
        if name == "halo":
            own_a.wait()
            arrive("hz")
            start("a1m", "a1p", "a20m", "a20p")
            return
        if name[0] == "E":
            start("e" + name[1:], "f" + name[1:])
            return
        if name[0] == "X":
            arrive("e" + name[1:], "f" + name[1:])
            return
        if name[:2] == "wb":
            if name == "wb0":
                own_w[0].wait()
                own_w[1].wait()
            arrive(*[f"{name}q{q}" for q in range(4)])
            return
        arrive(name)
        if name[:2] == "wx":
            q = int(name[2]) * 2 + 1
            start(f"wp1q{q}", f"ws1q{q}", f"wb0q{q}")
        elif name[0] == "w":
            j, q = int(name[2]), name[4]
            if j < (4 if name[1] == "p" else 3):
                start(f"w{name[1]}{j + 1}q{q}")
            start(f"wb{j if name[1] == 'p' else j + 4}q{q}")
        elif name in ("a1m", "a1p"):
            u = 1 if name == "a1m" else 2
            start(f"a1h{name[2]}", f"a2{u}m", f"a2{u}p")
        elif name == "a1hm":
            start("a23m", "a23p")
        elif name[:2] == "a2" and len(name) == 4:
            start(f"{name[:3]}h{name[3]}")

    barrier = pltpu.get_barrier_semaphore()
    peers = [sibling, partner, z_next, z_prev, first(1), first(-1), second(1), second(-1), across]
    for peer in peers:
        pl.semaphore_signal(barrier, inc=1, device_id=peer, device_id_type=MESH)
    pl.semaphore_wait(barrier, len(peers))

    start("hz", "wx0", "wx1", "wp1q0", "ws1q0", "wp1q2", "ws1q2")
    own_a.start()
    own_w[0].start()
    own_w[1].start()
    start("wb0q0", "wb0q2")

    @pl.loop(0, 24)
    def _(r):
        m = pl.ds(pl.multiple_of(r * WIDE, WIDE), WIDE)
        acc[:, m, :] = jnp.zeros((3, WIDE, 256), jnp.float32)

    @pl.loop(0, 16)
    def _(s):
        abuf[s // 8, s % 8, 0] = jnp.zeros((WIDE, 256), jnp.bfloat16)

    keys = []
    for k in range(8):
        dz, dx, dy = (k - z + 8) % 8, (k // 2 - x + 4) % 4, (k + y) % 2
        far = jnp.where(dz > 4, 8 - dz, dz)
        filters = sum(jnp.where(far == j, FILTERS_AT[j], 0) for j in range(5))
        blocks = sum(
            jnp.where((dx == int(chunk[0])) & (dy == int(chunk[1])), group_of("X" + chunk), 0) for chunk in CHUNKS)
        keys.append(jnp.maximum(filters, blocks) * 8 + k)
    ranks = [sum(jnp.where(other < key, 1, 0) for other in keys) for key in keys]
    ordered = [sum(jnp.where(rank == i, key, 0) for rank, key in zip(ranks, keys)) for i in range(8)]

    def operands_of(k, block):
        def operand(a):
            picked = []
            for r in range(12):
                g = ((z * 2 + block) * 2 + c) * 12 + r
                at, row = block, r + a
                if a == 0:
                    if r == 0:
                        at, row = jnp.where(block == 0, 1 - c, 1), jnp.where(block == 0, 13 + c, 14)
                    row = jnp.where(g % SIDE == 0, 0, row)
                if a == 2:
                    if r == 11:
                        at, row = jnp.where(block == 0, 0, 1 - c), jnp.where(block == 0, 15, 15 - 2 * c)
                    row = jnp.where(((g + 1) % SIDE == 0) | (g + 1 == ROWS), 0, row)
                picked.append(abuf[at, k, row])
            return jnp.concatenate(picked, axis=0)

        return [operand(a) for a in range(3)]

    def rows_of(block):
        return pl.ds(pl.multiple_of(block * 12 * WIDE, WIDE), 12 * WIDE)

    def dots(operands, weights):
        total = jnp.dot(operands[0], weights(0), preferred_element_type=jnp.float32)
        total += jnp.dot(operands[1], weights(1), preferred_element_type=jnp.float32)
        total += jnp.dot(operands[2], weights(2), preferred_element_type=jnp.float32)
        return total

    def compute(k, block):
        operands, m = operands_of(k, block), rows_of(block)
        for b in range(3):
            acc[b, m] += dots(operands, lambda a: jnp.concatenate([wbuf[k, n, a, b] for n in range(2)], axis=1))

    def compute_last(k, block, n):
        operands, m = operands_of(k, block), rows_of(block)
        total = dots(operands, lambda a: jnp.concatenate([wbuf[k, n, a, b] for b in range(3)], axis=1))
        for b in range(3):
            acc[b, m, columns(0, n)] += total[:, b * 128 : b * 128 + 128]

    column = lax.broadcasted_iota(jnp.int32, (WIDE, 128), 0)

    def finish(place, block, n):
        bias = b_ref[:, columns(yh, n)]

        @pl.loop(0, 12, unroll=3)
        def _(r):
            m = pl.ds(pl.multiple_of((block * 12 + r) * WIDE, WIDE), WIDE)
            left = jnp.where(column == 0, 0.0, pltpu.roll(acc[0, m, columns(0, n)], 1, 0))
            right = jnp.where(column == SIDE - 1, 0.0, pltpu.roll(acc[2, m, columns(0, n)], WIDE - 1, 0))
            value = acc[1, m, columns(0, n)] + left + right + bias
            ost[place, n, r] = value[:SIDE].astype(jnp.bfloat16)

    def dispatch(step, lo, hi):
        if hi - lo == 1:
            for name in GROUPS[lo].split():
                event(name)
            return
        mid = (lo + hi) // 2

        @pl.when(step < mid)
        def _():
            dispatch(step, lo, mid)

        @pl.when(step >= mid)
        def _():
            dispatch(step, mid, hi)

    def turn(step, done):
        @pl.when(step < len(GROUPS))
        def _():
            dispatch(step, 0, len(GROUPS))

        key = sum(jnp.where(done // 2 == i, ordered[i], 0) for i in range(8))
        ready = (done < 14) & (key // 8 <= step)

        @pl.when(ready)
        def _():
            compute(key % 8, jnp.where(done % 2 == 0, 1 - yh, yh))

        return done + jnp.where(ready, 1, 0)

    lax.fori_loop(0, len(GROUPS) + 13, turn, 0)

    outs = [pltpu.make_async_copy(ost.at[1, n], rows_out(yh, n), local_sem.at[3 + n]) for n in range(2)]

    @pl.loop(0, 4)
    def _(t):
        n, place = t % 2, t // 2

        @pl.when(t == 0)
        def _():
            arrive("wb4q0", "wb4q1")

        @pl.when(t == 1)
        def _():
            event("wp4q3")
            arrive("wb4q2", "wb4q3")

        block = jnp.where(place == 0, 1 - yh, yh)
        compute_last((z + 4) % 8, block, n)
        finish(place, block, n)
        for i in range(2):

            @pl.when(t == i)
            def _():
                start(f"o{i}")

            @pl.when(t == i + 2)
            def _():
                outs[i].start()

    for name in NAMES:
        if name[0] != "o":
            copy(name).wait_send()
    outs[0].wait()
    outs[1].wait()
    arrive("o0", "o1")
    copy("o0").wait_send()
    copy("o1").wait_send()


def local(activations, filters, channel_bias):
    out_local = filters.shape[3]
    return pl.pallas_call(
        kernel,
        out_shape=jax.ShapeDtypeStruct((12, SIDE, out_local), jnp.bfloat16),
        in_specs=[
            pl.BlockSpec(memory_space=pl.ANY),
            pl.BlockSpec(memory_space=pl.ANY),
            pl.BlockSpec(memory_space=pltpu.VMEM),
        ],
        out_specs=pl.BlockSpec(memory_space=pl.ANY),
        scratch_shapes=[
            pltpu.VMEM((2, 8, 16, WIDE, 256), jnp.bfloat16),
            pltpu.VMEM((8, 2, 3, 3, 256, 128), jnp.bfloat16),
            pltpu.VMEM((3, 24 * WIDE, 256), jnp.float32),
            pltpu.VMEM((2, 2, 12, SIDE, 128), jnp.bfloat16),
            pltpu.SemaphoreType.DMA((len(NAMES),)),
            pltpu.SemaphoreType.DMA((len(NAMES),)),
            pltpu.SemaphoreType.DMA((5,)),
        ],
        compiler_params=pltpu.CompilerParams(collective_id=0, has_side_effects=True),
    )(activations, filters, channel_bias.reshape(1, out_local))


def solution(mesh):
    placed = (P("img", None, "ch"), P(None, None, "img", "ch"), P("ch"))
    return jax.shard_map(
        local, mesh=mesh, in_specs=placed, out_specs=P("img", None, "ch"), check_vma=False
    )
```
